32 devices in a mesh: ctx: 8 (over z, x), exp: 4 (over y, core).
Axes of the slice: x: 2, y: 2, z: 4, core: 2. Of those that a mesh axis runs over, the one named last changes fastest.
Arguments:
- tokens: bfloat16 [2, 1024, 4096], P(None, 'ctx'), may hold values from -1.5 to 1.5
- router: bfloat16 [4096, 2048], P('ctx', 'exp'), may hold values from -8 to 8
- slot_out: bfloat16 [2, 2048, 4096], P(None, 'exp', 'ctx'), may hold values from -6 to 6
- out_grad: bfloat16 [2, 1024, 4096], P(None, 'ctx'), may hold values from -3 to 3
- slot_in_grad: bfloat16 [2, 2048, 4096], P(None, 'exp', 'ctx'), may hold values from -60 to 60
- lengths: int32 [2], replicated, may hold values from 256 to 1024, as said below
Outputs:
- grad_tokens: bfloat16 [2, 1024, 4096], P(None, 'ctx', 'exp')
- grad_router: float32 [4096, 2048], P('ctx', 'exp')
The draws below stay inside these ranges and needn't reach their ends.
Inputs may be any that keep to these rules, and one draw needn't show every extreme that they name: `lengths`: at least one sequence is valid at all 1024 positions.
All inputs are finite; a program needn't handle non-finite values.
Results may differ from the reference program's by a relative error of at most 0.017.
Values may be sent and summed in bfloat16 or wider, within the bound.
No kernel may reach another device: no remote copies, remote signals or barrier semaphores. Data moves between devices by JAX's collectives and lax.ppermute only.
A program may use at most 64 MiB of HBM per device.

```python
import math
import jax
import jax.numpy as jnp
from jax import lax

D = 4096
SEQS = 2
SLOTS = 2048
LENGTH = 1024
N_EXP = 4


def draw_tokens(key, part):
    base_key = jax.random.fold_in(key, 11)
    return jnp.clip(jax.random.normal(base_key, (SEQS, LENGTH, D)) * 0.125, -0.75, 0.75).astype(jnp.bfloat16)


def draw_router(key, part):
    base_key = jax.random.fold_in(key, 13)
    spread = 16.0 / math.sqrt(D)
    return jnp.clip(jax.random.normal(base_key, (D, SLOTS)) * spread, -8.0, 8.0).astype(jnp.bfloat16)


def draw_lengths(key, part):
    keys = jax.random.split(jax.random.fold_in(key, 17), 2)
    shorter = jax.random.randint(keys[0], (SEQS,), LENGTH // 4, LENGTH)
    full_seq = jax.random.randint(keys[1], (), 0, SEQS)
    return jnp.where(jnp.arange(SEQS) == full_seq, LENGTH, shorter).astype(jnp.int32)


def levels(key, extent, shards, least, largest):
    level, own = 1.0, jax.random.fold_in(key, 6)
    for dim, blocks in shards:
        draws = jnp.exp(jax.random.uniform(jax.random.fold_in(own, dim), (blocks,), jnp.float32, least / len(shards), largest / len(shards)))
        level = level * jnp.repeat(draws, extent[dim] // blocks).reshape([-1 if axis == dim else 1 for axis in range(len(extent))])
    return level


def bell_draw(key, dims, scale, reach, shards=(), kind=jnp.bfloat16):
    factor_of = levels(key, dims, shards, -0.22, 0.18) if shards else 1.0
    drawn = jax.random.normal(key, dims, jnp.float32) * scale * factor_of
    return jnp.minimum(jnp.maximum(drawn, -reach), reach).astype(kind)


def setup_inputs(seed: int = 0) -> dict:
    splits = jax.random.split(jax.random.key(seed), 7)
    tokens = draw_tokens(jax.random.fold_in(splits[6], 71), 0)
    router = draw_router(jax.random.fold_in(splits[6], 71), 0)
    slot_out = bell_draw(splits[2], (SEQS, SLOTS, D), 1.0, 6.0, ((1, 4), (2, 8)))
    out_grad = bell_draw(splits[3], (SEQS, LENGTH, D), 0.5, 3.0, ((1, 8),))
    slot_in_grad = bell_draw(splits[4], (SEQS, SLOTS, D), 10.0, 60.0, ((1, 4), (2, 8)))
    lengths = draw_lengths(jax.random.fold_in(splits[6], 71), 0)
    return {"tokens": tokens, "router": router, "slot_out": slot_out, "out_grad": out_grad, "slot_in_grad": slot_in_grad, "lengths": lengths}


masked_logit = -1e30


def round_low(values):
    return lax.optimization_barrier(values.astype(jnp.bfloat16)).astype(jnp.float32)


def reference(tokens, router, slot_out, out_grad, slot_in_grad, lengths):
    positions = jnp.arange(LENGTH, dtype=jnp.int32)
    valid_mask = positions[None, :] < lengths[:, None]
    tokens_high = tokens.astype(jnp.float32)
    router_high = router.astype(jnp.float32)
    logits = jnp.einsum("bnd,ds->bns", tokens_high, router_high)
    combine = jax.nn.softmax(logits, axis=2)
    grad_in = jnp.where(valid_mask[:, :, None], out_grad.astype(jnp.float32), jnp.float32(0.0))
    comb_grad = jnp.einsum("bnd,bsd->bns", grad_in, slot_out.astype(jnp.float32))
    comb_mean = jnp.sum(combine * comb_grad, axis=2, keepdims=True)
    masked = jnp.where(valid_mask[:, :, None], logits, jnp.float32(masked_logit))
    peaks = jnp.max(masked, axis=1, keepdims=True)
    shifted = jnp.where(valid_mask[:, :, None], jnp.exp(masked - peaks), jnp.float32(0.0))
    dispatch = shifted / jnp.sum(shifted, axis=1, keepdims=True)
    grads_high = slot_in_grad.astype(jnp.float32)
    disp_grad = jnp.einsum("bnd,bsd->bns", tokens_high, grads_high)
    disp_mean = jnp.sum(dispatch * disp_grad, axis=1, keepdims=True)
    grad_logits = combine * (comb_grad - comb_mean) + dispatch * (disp_grad - disp_mean)
    logit_low = round_low(grad_logits)
    dispatch_low = round_low(dispatch)
    grad_router = jnp.einsum("bnd,bns->ds", tokens_high, logit_low)
    group_width = SLOTS // N_EXP
    grad_sum = jnp.zeros(tokens.shape, jnp.float32)
    for group_index in range(N_EXP):
        slot_low = group_index * group_width
        slot_high = slot_low + group_width
        group_part = jnp.einsum("bns,bsd->bnd", dispatch_low[:, :, slot_low:slot_high], grads_high[:, slot_low:slot_high])
        group_part = group_part + jnp.einsum("bns,ds->bnd", logit_low[:, :, slot_low:slot_high], router_high[:, slot_low:slot_high])
        grad_sum = grad_sum + round_low(group_part)
    return grad_sum.astype(jnp.bfloat16), grad_router
```

```python
import jax
import jax.numpy as jnp
from jax import lax
from jax.sharding import Mesh
from jax.sharding import PartitionSpec as P

masked_logit = -1e30
low = jnp.bfloat16


def flip(value, axis, bits):
    size = lax.axis_size(axis)
    return lax.ppermute(value, axis, [(i, i ^ bits) for i in range(size)])


def powers(size):
    return [1 << k for k in range(size.bit_length() - 1)]


def by_bit(bit, own, other, axis):
    first = jnp.where(bit == 0, own, other)
    second = jnp.where(bit == 0, other, own)
    return jnp.stack([first, second], axis=axis)


def merge(one, two):
    peak = jnp.maximum(one[0], two[0])
    left, right = jnp.exp(one[0] - peak), jnp.exp(two[0] - peak)
    return jnp.stack([peak, one[1] * left + two[1] * right, one[2] * left + two[2] * right])


def local(tokens, router, slot_out, out_grad, slot_in_grad, lengths):
    seqs, rows, width = tokens.shape
    part, slots = router.shape
    zs, ys = lax.axis_size("z"), lax.axis_size("y")
    zi, xi, yi, ci = (lax.axis_index(a) for a in ("z", "x", "y", "c"))
    wide = 2 * part
    groups = 2 * ys
    piece = seqs * rows // groups
    half = rows // 2
    rel = range(zs)

    positions = (zi * 2 + xi) * rows + jnp.arange(rows, dtype=jnp.int32)
    valid = (positions[None, :] < lengths[:, None])[:, :, None]

    def spread(flat):
        mine = lax.dynamic_slice(flat, ((yi * 2 + ci) * piece, 0), (piece, width))
        out = []
        for j in rel:
            block = lax.dynamic_slice(mine, (0, (zi ^ j) * wide), (piece, wide))
            out.append(block if j == 0 else flip(block, "z", j))
        held = jnp.stack(out)[None]
        for bit in powers(ys):
            other = flip(held, "y", bit)
            held = by_bit((yi // bit) % 2, held, other, 0).reshape((-1,) + held.shape[1:])
        held = by_bit(ci, held, flip(held, "c", 1), 1)
        held = held.reshape(seqs, groups // seqs, zs, piece, wide)
        return held.transpose(0, 2, 1, 3, 4).reshape(seqs, zs * rows, wide)

    def joined(own):
        other = flip(own, "x", 1)
        return jnp.concatenate(
            [jnp.where(xi == 0, own, other), jnp.where(xi == 0, other, own)], axis=-1
        )

    def reduced(product):
        blocks = product.reshape(seqs, zs, rows, slots)
        total = blocks[:, 0]
        for j in rel[1:]:
            total = total + flip(blocks[:, j].astype(low), "z", j).astype(jnp.float32)
        return total

    def gathered(mine):
        return jnp.stack([mine] + [flip(mine, "z", j) for j in rel[1:]], axis=1).reshape(
            seqs, zs * rows, slots
        )

    pieces = {0: router}
    for bit in reversed(powers(zs)):
        pieces.update({j ^ bit: flip(pieces[j], "z", bit) for j in list(pieces)})
    ordered = []
    for j in rel:
        other = flip(pieces[j], "x", 1)
        ordered += [jnp.where(xi == 0, pieces[j], other), jnp.where(xi == 0, other, pieces[j])]
    phi = jnp.concatenate(ordered, axis=0)

    flat_tokens = tokens.reshape(seqs * rows, width)
    masked_grad = jnp.where(valid, out_grad, jnp.zeros((), out_grad.dtype))
    tok = spread(flat_tokens)
    out_g = spread(masked_grad.reshape(seqs * rows, width))
    sig = joined(slot_in_grad)
    outs = joined(slot_out)

    disp_grad = reduced(jnp.einsum("bnd,bsd->bns", tok, sig, preferred_element_type=jnp.float32))
    comb_grad = reduced(jnp.einsum("bnd,bsd->bns", out_g, outs, preferred_element_type=jnp.float32))

    turned = jnp.concatenate(
        [lax.dynamic_slice(flat_tokens, (0, (zi ^ j) * wide), (seqs * rows, wide)) for j in rel], axis=1
    )
    logits = jnp.dot(turned, phi, preferred_element_type=jnp.float32).reshape(seqs, rows, slots)

    masked = jnp.where(valid, logits, masked_logit)
    slot_peak = jnp.max(masked, axis=1)
    slot_shift = jnp.where(valid, jnp.exp(masked - slot_peak[:, None, :]), 0.0)
    disp = jnp.stack([slot_peak, jnp.sum(slot_shift, axis=1), jnp.sum(slot_shift * disp_grad, axis=1)])
    disp = merge(disp, flip(disp, "x", 1))
    for bit in powers(zs):
        disp = merge(disp, flip(disp, "z", bit))

    peak = jnp.max(logits, axis=2)
    shifted = jnp.exp(logits - peak[:, :, None])
    comb = jnp.stack([peak, jnp.sum(shifted, axis=2), jnp.sum(shifted * comb_grad, axis=2)])
    comb = merge(comb, flip(comb, "c", 1))
    for bit in powers(ys):
        comb = merge(comb, flip(comb, "y", bit))

    dispatch = jnp.where(
        valid, jnp.exp(masked - disp[0][:, None, :]) / disp[1][:, None, :], 0.0
    )
    dispatch_low = dispatch.astype(low)
    combine = jnp.exp(logits - comb[0][:, :, None]) / comb[1][:, :, None]
    grad_logits = combine * (comb_grad - (comb[2] / comb[1])[:, :, None]) + dispatch * (
        disp_grad - (disp[2] / disp[1])[:, None, :]
    )
    logit_low = grad_logits.astype(low)

    dispatch_all = gathered(dispatch_low)
    share = jnp.einsum("bns,bsd->bnd", dispatch_all, sig, preferred_element_type=jnp.float32)
    share = share.reshape(seqs, zs, 2, half, wide)

    def mine_of(value, axis):
        return lax.dynamic_index_in_dim(value, ci, axis, keepdims=False)

    def other_of(value, axis):
        return lax.dynamic_index_in_dim(value, 1 - ci, axis, keepdims=False)

    share = mine_of(share, 2) + flip(other_of(share, 2).astype(low), "c", 1).astype(jnp.float32)
    share_low = share.astype(low)
    from_disp = jnp.stack(
        [share_low[:, 0]] + [flip(share_low[:, j], "z", j) for j in rel[1:]], axis=2
    )

    logit_all = gathered(logit_low)
    partial_router = jnp.einsum("bnd,bns->ds", tok, logit_all, preferred_element_type=jnp.float32)
    partial_router = partial_router.reshape(2, part, slots)
    grad_router = lax.dynamic_index_in_dim(partial_router, xi, 0, keepdims=False) + flip(
        lax.dynamic_index_in_dim(partial_router, 1 - xi, 0, keepdims=False).astype(low), "x", 1
    ).astype(jnp.float32)

    whole = jnp.einsum("bns,ds->bnd", logit_low, phi, preferred_element_type=jnp.float32)
    whole = whole.reshape(seqs, 2, half, zs, wide)
    whole = (
        mine_of(whole, 1)
        + flip(other_of(whole, 1).astype(low), "c", 1).astype(jnp.float32)
        + from_disp.astype(jnp.float32)
    )

    def blocks_of(y):
        return jnp.stack(
            [lax.dynamic_index_in_dim(whole, (2 * y + c) ^ zi, 2, keepdims=False) for c in range(2)]
        )

    final = blocks_of(yi)
    for t in range(1, ys):
        final = final + flip(blocks_of(yi ^ t).astype(low), "y", t).astype(jnp.float32)
    final = final.astype(low)
    kept, got = mine_of(final, 0), flip(other_of(final, 0), "c", 1)
    grad_tokens = by_bit(ci, kept, got, 1).reshape(seqs, rows, wide)
    return grad_tokens, grad_router


def solution(mesh):
    ctx, exp = mesh.shape["ctx"], mesh.shape["exp"]
    assert ctx // 2 == exp
    inner = Mesh(mesh.devices.reshape(ctx // 2, 2, exp // 2, 2), ("z", "x", "y", "c"))
    ctx_axes, exp_axes = ("z", "x"), ("y", "c")
    return jax.shard_map(
        local,
        mesh=inner,
        in_specs=(
            P(None, ctx_axes, None),
            P(ctx_axes, exp_axes),
            P(None, exp_axes, ctx_axes),
            P(None, ctx_axes, None),
            P(None, exp_axes, ctx_axes),
            P(),
        ),
        out_specs=(P(None, ctx_axes, exp_axes), P(ctx_axes, exp_axes)),
        check_vma=False,
    )
```
